32 devices in a mesh: loop: 16 (over z, x, core), ch: 2 (over y).
Axes of the slice: x: 2, y: 2, z: 4, core: 2. Of those that a mesh axis runs over, the one named last changes fastest.
Arguments:
- genome: bfloat16 [8192, 1536], P('loop', 'ch'), may hold values from -6 to 6
- dilated_kernel_weight: bfloat16 [2, 3, 1536, 768], P(None, None, 'ch', 'loop'), may hold values from -0.09375 to 0.09375
- pointwise_weight: bfloat16 [2, 768, 1536], P(None, 'loop', 'ch'), may hold values from -0.21875 to 0.21875
- bottleneck_scale: float32 [2, 768], replicated, may hold values from 0.5 to 2
- bottleneck_shift: float32 [2, 768], replicated, may hold values from -3 to 3
- output_scale: float32 [2, 1536], P(None, 'ch'), may hold values from 0.3 to 1.5
- output_shift: float32 [2, 1536], P(None, 'ch'), may hold values from -2 to 2
Outputs:
- trunk_out: bfloat16 [8192, 1536], P('loop', 'ch')
The draws below stay inside these ranges and needn't reach their ends.
All inputs are finite; a program needn't handle non-finite values.
Results may differ from the reference program's by a relative error of at most 0.008.
Values may be sent and summed in bfloat16 or wider, within the bound.
A program may use at most 64 MiB of HBM per device.

```python
import math
import jax
import jax.numpy as jnp

C = 1536
B = 768
POSITIONS = 8192
FIRST_DILATION = 512
SECOND_DILATION = 1024


def block_scale(key, dims, pieces, low, top_value):
    gain = 1.0
    for dim, parts in pieces:
        heights = jax.random.uniform(jax.random.fold_in(jax.random.fold_in(key, 6), dim), (parts,), jnp.float32, low / len(pieces), top_value / len(pieces))
        gain = gain * jnp.repeat(jnp.exp(heights), dims[dim] // parts).reshape((-1,) + (1,) * (len(dims) - 1 - dim))
    return gain


def noise(key, dims, spread, reach, pieces=(), kind=jnp.bfloat16):
    result = jax.random.normal(key, dims, jnp.float32) * spread
    if len(pieces) > 0:
        result = block_scale(key, dims, pieces, -0.22, 0.18) * result
    return jnp.clip(result, min=-reach, max=reach).astype(kind)


def setup_inputs(seed: int = 0) -> dict:
    key_list = jax.random.split(jax.random.key(seed), 8)
    return {
        "genome": noise(key_list[0], (POSITIONS, C), 1.0, 6.0, ((0, 16), (1, 2))),
        "dilated_kernel_weight": noise(key_list[1], (2, 3, C, B), (3 * C) ** -0.5, 0.09375, ((2, 2), (3, 16))),
        "pointwise_weight": noise(key_list[2], (2, B, C), B ** -0.5, 0.21875, ((1, 16), (2, 2))),
        "bottleneck_scale": jnp.clip(jnp.exp(jax.random.uniform(key_list[3], (2, B), jnp.float32, math.log(0.5), math.log(2.0))), 0.5, 2.0),
        "bottleneck_shift": noise(key_list[4], (2, B), 0.5, 3.0, (), jnp.float32),
        "output_scale": jnp.clip(jnp.exp(math.log(1.5) - 1.60943787 * jax.random.uniform(key_list[5], (2, C), jnp.float32) ** block_scale(key_list[5], (2, C), ((1, 2),), -0.2, 0.2)), 0.3, 1.5),
        "output_shift": noise(key_list[6], (2, C), 0.3, 2.0, ((1, 2),), jnp.float32),
    }


def apply_residual_block(trunk_state, conv_kernels, projection, scale_mid, shift_mid, scale_out, shift_out, dilation):
    activated = jax.nn.gelu(trunk_state.astype(jnp.float32)).astype(jnp.bfloat16)
    before_taps = jnp.roll(activated, dilation, axis=0)
    after_taps = jnp.roll(activated, -dilation, axis=0)
    middle = jnp.dot(before_taps, conv_kernels[0], preferred_element_type=jnp.float32)
    middle = middle + jnp.dot(activated, conv_kernels[1], preferred_element_type=jnp.float32)
    middle = middle + jnp.dot(after_taps, conv_kernels[2], preferred_element_type=jnp.float32)
    hidden_act = jax.nn.gelu(middle * scale_mid + shift_mid).astype(jnp.bfloat16)
    projected = jnp.dot(hidden_act, projection, preferred_element_type=jnp.float32)
    updated = trunk_state.astype(jnp.float32) + projected * scale_out + shift_out
    return updated.astype(jnp.bfloat16)


def reference(genome, dilated_kernel_weight, pointwise_weight, bottleneck_scale, bottleneck_shift, output_scale, output_shift):
    trunk_state = apply_residual_block(genome, dilated_kernel_weight[0], pointwise_weight[0], bottleneck_scale[0], bottleneck_shift[0], output_scale[0], output_shift[0], FIRST_DILATION)
    trunk_state = apply_residual_block(trunk_state, dilated_kernel_weight[1], pointwise_weight[1], bottleneck_scale[1], bottleneck_shift[1], output_scale[1], output_shift[1], SECOND_DILATION)
    return trunk_state
```

```python
import functools

import jax
import jax.numpy as jnp
from jax import lax
from jax.experimental import pallas as pl
from jax.experimental.pallas import tpu as pltpu
from jax.sharding import PartitionSpec as P

MESH = pl.DeviceIdType.MESH
CORES = 2
TILE = 16
PIECES = 2
VMEM_BYTES = 67043328
TO_OUTER = ((1, 0),)
TO_INNER = ((0, 1), (1, 0), (1, 1))
HALVES = 2


def gelu(v):
    return 0.5 * v * (1.0 + jnp.tanh(0.7978845608028654 * (v + 0.044715 * (v * v * v))))


def from_behind(x, axis, by):
    peers = lax.axis_size(axis)
    return lax.ppermute(x, axis, [(i, (i + by) % peers) for i in range(peers)])


def plain_shards(genome, kernel_w, point_w, mid_scale, mid_shift, out_scale, out_shift):
    state = genome
    for b in range(2):
        act = jax.nn.gelu(state.astype(jnp.float32)).astype(jnp.bfloat16)
        before = from_behind(act, "loop", b + 1)
        after = from_behind(act, "loop", -(b + 1))
        kernels = lax.all_gather(kernel_w[b], "loop", axis=2, tiled=True)
        projection = lax.all_gather(point_w[b], "loop", axis=0, tiled=True)
        mid = jnp.dot(before, kernels[0], preferred_element_type=jnp.float32)
        mid = mid + jnp.dot(act, kernels[1], preferred_element_type=jnp.float32)
        mid = mid + jnp.dot(after, kernels[2], preferred_element_type=jnp.float32)
        mid = lax.psum(mid, "ch")
        hid = jax.nn.gelu(mid * mid_scale[b] + mid_shift[b]).astype(jnp.bfloat16)
        proj = jnp.dot(hid, projection, preferred_element_type=jnp.float32)
        state = (state.astype(jnp.float32) + proj * out_scale[b] + out_shift[b]).astype(jnp.bfloat16)
    return state


def kernel(
    peers, xs, x_ref, k_ref, p_ref, ms_ref, mt_ref, os_ref, ot_ref, o_ref,
    state, act, wbuf, mid, psend, precv, acc, res, cols, coef, lmid, lsend, lrecv,
    in_s, in_r, out_s, out_r, wr, wp, wx, wu, wd, wq, we, ys, yr, yls, ylr, loc,
):
    rows, width = x_ref.shape
    part = rows // peers
    slab = p_ref.shape[1]
    zs = peers // (CORES * xs)
    chunk = slab * CORES * xs
    me = lax.axis_index("loop")
    half = lax.axis_index("ch")
    c = lax.rem(me, CORES)
    x = lax.rem(me // CORES, xs)
    z = me // (CORES * xs)
    pad = 2 * part

    def rowset(i):
        return pl.ds(pl.multiple_of(i * part, part), part)

    def a2a_in(to):
        return pltpu.make_async_remote_copy(
            src_ref=x_ref.at[rowset(to)], dst_ref=state.at[rowset(me)],
            send_sem=in_s.at[to], recv_sem=in_r.at[me],
            device_id={"loop": to}, device_id_type=MESH)

    def a2a_in_recv(i):
        frm = lax.rem(me + i, peers)
        return pltpu.make_async_remote_copy(
            src_ref=x_ref.at[rowset(frm)], dst_ref=state.at[rowset(frm)],
            send_sem=in_s.at[frm], recv_sem=in_r.at[frm],
            device_id={"loop": frm}, device_id_type=MESH)

    def a2a_out(to):
        return pltpu.make_async_remote_copy(
            src_ref=res.at[rowset(to)], dst_ref=o_ref.at[rowset(me)],
            send_sem=out_s.at[to], recv_sem=out_r.at[me],
            device_id={"loop": to}, device_id_type=MESH)

    def a2a_out_recv(i):
        frm = lax.rem(me + i, peers)
        return pltpu.make_async_remote_copy(
            src_ref=res.at[rowset(frm)], dst_ref=o_ref.at[rowset(frm)],
            send_sem=out_s.at[frm], recv_sem=out_r.at[frm],
            device_id={"loop": frm}, device_id_type=MESH)

    def plane(s):
        low = jnp.where(z < zs // 2, z, zs - 1 - z)
        at = jnp.where(s <= low, low - s, s)
        return jnp.where(z < zs // 2, at, zs - 1 - at)

    def to_all(copy, prepare=None):
        group = CORES * xs
        spot = lax.rem(me, group)

        @pl.loop(0, zs - 1)
        def _(k):
            base = lax.rem(z + 1 + k, zs) * group
            if prepare is not None:
                prepare(base, group)
            for j in range(group):
                copy(base + lax.rem(spot + j, group)).start()

        if prepare is not None:
            prepare(z * group, group)
        for j in range(1, group):
            copy(z * group + lax.rem(spot + j, group)).start()

    def index(zi, xi, ci):
        return (zi * xs + xi) * CORES + ci

    def place(b, h, owner):
        return wbuf.at[b, pl.ds(h * (4 // PIECES), 4 // PIECES), pl.ds(pl.multiple_of(owner * slab, slab), slab), :]

    def wcopy(b, h, owner, to, sem):
        return pltpu.make_async_remote_copy(
            src_ref=place(b, h, owner),
            dst_ref=place(b, h, owner),
            send_sem=sem, recv_sem=wr.at[b, h, owner],
            device_id={"loop": to}, device_id_type=MESH)

    def got(b, h, owner):
        wcopy(b, h, owner, lax.rem(me + 1, peers), wp.at[b, h, 0]).wait_recv()

    def along(b, h, s, act_on):
        zp = plane(s)
        owner = index(zp, x, c)

        @pl.when((zp <= z) & (z < zs - 1))
        def _():
            act_on(wcopy(b, h, owner, index(lax.rem(z + 1, zs), x, c), wu.at[b, h, s]))

        @pl.when((zp >= z) & (z > 0))
        def _():
            act_on(wcopy(b, h, owner, index(lax.rem(z + zs - 1, zs), x, c), wd.at[b, h, s]))

    edge = jnp.where(z % 2 == 0, z + 1, z - 1)
    outer = (z == 0) | (z == zs - 1)

    def by_edge(b, h, corner):
        return (b, h) in (TO_INNER if corner else TO_OUTER)

    def over_x(b, h, s):
        may = not isinstance(s, int) or s == 1
        skip_outer = may and by_edge(b, h, False)
        skip_inner = may and by_edge(b, h, True)
        keep = z >= 0
        if skip_outer:
            keep = keep & jnp.logical_not(outer & (s == 1))
        if skip_inner:
            keep = keep & (outer | (s != 1))
        return keep

    def across(b, h, s, act_on):
        owner = index(plane(s), x, c)

        @pl.when(over_x(b, h, s))
        def _():
            for j in range(1, xs):
                act_on(wcopy(b, h, owner, index(z, lax.rem(x + j, xs), c), wx.at[b, h, s * (xs - 1) + j - 1]))

        act_on(wcopy(b, h, owner, index(z, x, 1 - c), wp.at[b, h, s]))

    def past_edge(b, h, act_on):
        if not by_edge(b, h, True) and not by_edge(b, h, False):
            return
        copy = wcopy(b, h, index(z, 1 - x, c), index(edge, x, c), we.at[b, h])
        if by_edge(b, h, True):
            @pl.when(outer)
            def _():
                act_on(copy)
        if by_edge(b, h, False):
            @pl.when(jnp.logical_not(outer))
            def _():
                act_on(copy)

    def start(copy):
        copy.start()

    def sent(copy):
        copy.wait_send()

    def forward_column(b, s):
        for h in range(PIECES):
            got(b, h, index(plane(s), x, c))
            along(b, h, s, start)
            across(b, h, s, start)

    def to_partner(b, h, s, j):
        owner = index(plane(s), lax.rem(x + j, xs), c)
        return wcopy(b, h, owner, index(z, x, 1 - c), wq.at[b, h, s * (xs - 1) + j - 1])

    def forward_across(b, s):
        for h in range(PIECES):
            for j in range(1, xs):
                got(b, h, index(plane(s), lax.rem(x + j, xs), c))

                @pl.when(s == 0)
                def _():
                    past_edge(b, h, start)

                to_partner(b, h, s, j).start()

    def arrived(b, s):
        for h in range(PIECES):
            for j in range(xs):
                got(b, h, index(plane(s), j, 1 - c))

    def ycopy(b, s):
        return pltpu.make_async_remote_copy(
            src_ref=psend.at[b, s], dst_ref=precv.at[b, s],
            send_sem=ys.at[b, s], recv_sem=yr.at[b, s],
            device_id={"ch": 1 - half}, device_id_type=MESH)

    def chunk_of(s):
        return pl.ds(pl.multiple_of(plane(s) * chunk, chunk), chunk)

    nt = (((1,), (1,)), ((), ()))
    tn = (((0,), (0,)), ((), ()))

    def middle(b, s):
        at = chunk_of(s)
        shift = (b + 1) * part
        total = None
        for t in range(3):
            term = lax.dot_general(
                wbuf[b, t, at, :], act[pl.ds(pad + (t - 1) * shift, rows), :], nt,
                preferred_element_type=jnp.float32)
            total = term if total is None else total + term
        mid[s] = total
        psend[b, s] = total.astype(jnp.bfloat16)
        ycopy(b, s).start()

    def project(b, s):
        at = chunk_of(s)
        ycopy(b, s).wait_recv()
        total = mid[s] + precv[b, s].astype(jnp.float32)
        hid = gelu(total * cols[at, pl.ds(b, 1)] + cols[at, pl.ds(2 + b, 1)]).astype(jnp.bfloat16)
        acc[...] += lax.dot_general(hid, wbuf[b, 3, at, :], tn, preferred_element_type=jnp.float32)

    step = 64 if rows % 64 == 0 else part

    def activate(src):
        @pl.loop(0, rows // step)
        def _(i):
            at = pl.ds(pl.multiple_of(i * step, step), step)
            act[pl.ds(pl.multiple_of(pad + i * step, part), step), :] = gelu(
                src[at, :].astype(jnp.float32)).astype(jnp.bfloat16)

        act[pl.ds(0, pad), :] = act[pl.ds(rows, pad), :]
        act[pl.ds(pad + rows, pad), :] = act[pl.ds(pad, pad), :]

    def update(b, src, dst):
        @pl.loop(0, rows // step)
        def _(i):
            at = pl.ds(pl.multiple_of(i * step, step), step)
            dst[at, :] = (
                src[at, :].astype(jnp.float32)
                + acc[at, :] * os_ref[pl.ds(b, 1), :] + ot_ref[pl.ds(b, 1), :]
            ).astype(jnp.bfloat16)

    def finish(first, count):
        at = pl.ds(pl.multiple_of(first * part, part), count * part)
        res[at, :] = (
            state[at, :].astype(jnp.float32) + acc[at, :] * os_ref[pl.ds(1, 1), :] + ot_ref[pl.ds(1, 1), :]
        ).astype(jnp.bfloat16)

    own_x = pltpu.make_async_copy(x_ref.at[rowset(me)], state.at[rowset(me)], loc.at[0])
    own_w = []
    for b in range(2):
        at = pl.ds(pl.multiple_of(me * slab, slab), slab)
        own_w.append(pltpu.make_async_copy(k_ref.at[b], wbuf.at[b, pl.ds(0, 3), at, :], loc.at[1 + 2 * b]))
        own_w.append(pltpu.make_async_copy(p_ref.at[b], wbuf.at[b, 3, at, :], loc.at[2 + 2 * b]))

    barrier = pltpu.get_barrier_semaphore()

    @pl.loop(1, peers)
    def _(i):
        pl.semaphore_signal(barrier, inc=1, device_id={"loop": lax.rem(me + i, peers)}, device_id_type=MESH)

    pl.semaphore_signal(barrier, inc=1, device_id={"ch": 1 - half}, device_id_type=MESH)
    for copy in own_w:
        copy.start()
    own_x.start()
    coef[...] = jnp.zeros_like(coef)
    coef[pl.ds(0, 2), :] = ms_ref[...]
    coef[pl.ds(2, 2), :] = mt_ref[...]
    cols[...] = coef[...].T
    acc[...] = jnp.zeros_like(acc)
    for copy in own_w:
        copy.wait()
    own_x.wait()
    pl.semaphore_wait(barrier, peers)

    def own_slab(b):
        for h in range(PIECES):
            along(b, h, 0, start)
            across(b, h, 0, start)

    inner = jnp.logical_not(outer)

    own_slab(0)
    to_all(a2a_in)
    forward_column(0, 1)

    @pl.when(outer)
    def _():
        own_slab(1)

    @pl.when(inner)
    def _():
        forward_column(0, 2)
        own_slab(1)

    @pl.loop(1, peers)
    def _(i):
        a2a_in_recv(i).wait_recv()

    activate(state)

    @pl.loop(0, zs + 1)
    def _(s):
        @pl.when(s < zs)
        def _():
            forward_across(0, s)
            arrived(0, s)
            middle(0, s)

        @pl.when(outer & (s == 0))
        def _():
            forward_column(0, 2)

        @pl.when((outer & (s == 2)) | (inner & (s == 1)))
        def _():
            forward_column(0, 3)

        @pl.when((outer & (s == 3)) | (inner & (s == 2)))
        def _():
            forward_column(1, 1)

        @pl.when(inner & (s == 3))
        def _():
            forward_column(1, 2)

        @pl.when(s > 0)
        def _():
            project(0, s - 1)

    update(0, state, state)
    activate(state)
    acc[...] = jnp.zeros_like(acc)

    @pl.loop(0, zs - 1)
    def _(s):
        forward_across(1, s)
        arrived(1, s)
        middle(1, s)

        @pl.when(outer & (s == 0))
        def _():
            forward_column(1, 2)

        @pl.when((outer & (s == 1)) | (inner & (s == 0)))
        def _():
            forward_column(1, 3)

        @pl.when(s > 0)
        def _():
            project(1, s - 1)

    project(1, zs - 2)
    last = zs - 1
    forward_across(1, last)
    arrived(1, last)
    group = CORES * xs
    level = group * part
    far = jnp.where(z < zs // 2, 1, 0)
    span = rows // HALVES
    last_at = chunk_of(last)
    shift = 2 * part

    def halfset(q):
        return pl.ds(pl.multiple_of(q * span, span), span)

    def lcopy(k):
        return pltpu.make_async_remote_copy(
            src_ref=lsend.at[k], dst_ref=lrecv.at[k],
            send_sem=yls.at[k], recv_sem=ylr.at[k],
            device_id={"ch": 1 - half}, device_id_type=MESH)

    def to_half(k):
        return jnp.where(far == 1, 1 - k, k) if HALVES == 2 else k

    for k in range(HALVES):
        q = to_half(k)
        total = None
        for t in range(3):
            term = lax.dot_general(
                wbuf[1, t, last_at, :],
                act[pl.ds(pl.multiple_of(pad + (t - 1) * shift + q * span, part), span), :], nt,
                preferred_element_type=jnp.float32)
            total = term if total is None else total + term
        lmid[k] = total
        lsend[k] = total.astype(jnp.bfloat16)
        lcopy(k).start()

    for k in range(HALVES):
        q = to_half(k)
        lcopy(k).wait_recv()
        total = lmid[k] + lrecv[k].astype(jnp.float32)
        hid = gelu(total * cols[last_at, pl.ds(1, 1)] + cols[last_at, pl.ds(3, 1)]).astype(jnp.bfloat16)
        acc[halfset(q), :] += lax.dot_general(hid, wbuf[1, 3, last_at, :], tn, preferred_element_type=jnp.float32)

        def send_level(zt):
            finish(zt * group, group)
            spot = lax.rem(me, group)
            for j in range(group):
                to = zt * group + lax.rem(spot + j, group)

                @pl.when(to != me)
                def _():
                    a2a_out(to).start()

        per = zs // HALVES

        @pl.loop(0, per)
        def _(i):
            at = jnp.where(z < zs // 2, per - 1 - i, i)
            send_level(q * per + at)

    own_o = pltpu.make_async_copy(res.at[rowset(me)], o_ref.at[rowset(me)], loc.at[0])
    own_o.start()
    own_o.wait()

    @pl.loop(1, peers)
    def _(i):
        a2a_out_recv(i).wait_recv()

    for b in range(2):
        for h in range(PIECES):
            along(b, h, 0, sent)
            across(b, h, 0, sent)
            past_edge(b, h, sent)

        @pl.loop(0, zs)
        def _(s):
            for h in range(PIECES):
                @pl.when(s > 0)
                def _():
                    along(b, h, s, sent)
                    across(b, h, s, sent)

                for j in range(1, xs):
                    to_partner(b, h, s, j).wait_send()

            @pl.when((s < zs - 1) | (b == 0))
            def _():
                ycopy(b, s).wait_send()

    for k in range(HALVES):
        lcopy(k).wait_send()

    @pl.loop(1, peers)
    def _(i):
        a2a_in(lax.rem(me + i, peers)).wait_send()
        a2a_out(lax.rem(me + i, peers)).wait_send()


def fused_shards(genome, kernel_w, point_w, mid_scale, mid_shift, out_scale, out_shift):
    peers = lax.axis_size("loop")
    rows, width = genome.shape
    slab = point_w.shape[1]
    mids = mid_scale.shape[1]
    xs = 2
    zs = peers // (CORES * xs)
    chunk = slab * CORES * xs
    part = rows // peers
    bf16, f32 = jnp.bfloat16, jnp.float32
    dma = pltpu.SemaphoreType.DMA
    hbm = pl.BlockSpec(memory_space=pltpu.HBM)
    vmem = pl.BlockSpec(memory_space=pltpu.VMEM)
    return pl.pallas_call(
        functools.partial(kernel, peers, xs),
        out_shape=jax.ShapeDtypeStruct((rows, width), bf16),
        in_specs=[hbm] * 3 + [vmem] * 4,
        out_specs=vmem,
        scratch_shapes=[
            pltpu.VMEM((rows, width), bf16),
            pltpu.VMEM((rows + 4 * part, width), bf16),
            pltpu.VMEM((2, 4, mids, width), bf16),
            pltpu.VMEM((zs, chunk, rows), f32),
            pltpu.VMEM((2, zs, chunk, rows), bf16),
            pltpu.VMEM((2, zs, chunk, rows), bf16),
            pltpu.VMEM((rows, width), f32),
            pltpu.VMEM((rows, width), bf16),
            pltpu.VMEM((mids, 8), f32),
            pltpu.VMEM((8, mids), f32),
            pltpu.VMEM((HALVES, chunk, rows // HALVES), f32),
            pltpu.VMEM((HALVES, chunk, rows // HALVES), bf16),
            pltpu.VMEM((HALVES, chunk, rows // HALVES), bf16),
            dma((peers,)), dma((peers,)), dma((peers,)), dma((peers,)),
            dma((2, PIECES, peers)), dma((2, PIECES, zs)), dma((2, PIECES, zs * (xs - 1))),
            dma((2, PIECES, zs)), dma((2, PIECES, zs)), dma((2, PIECES, zs * (xs - 1))),
            dma((2, PIECES)), dma((2, zs)), dma((2, zs)), dma((HALVES,)), dma((HALVES,)), dma((5,)),
        ],
        compiler_params=pltpu.CompilerParams(
            collective_id=0, has_side_effects=True, vmem_limit_bytes=VMEM_BYTES),
    )(genome, jnp.swapaxes(kernel_w, 2, 3), point_w, mid_scale, mid_shift, out_scale, out_shift)


def shards(genome, kernel_w, *rest):
    peers = lax.axis_size("loop")
    rows, width = genome.shape
    slab = kernel_w.shape[3]
    fits = (
        peers == CORES * 2 * 4 and rows % (peers * TILE) == 0 and slab % TILE == 0
        and width % 128 == 0 and rows % 128 == 0 and lax.axis_size("ch") == 2
    )
    return (fused_shards if fits else plain_shards)(genome, kernel_w, *rest)


def solution(mesh):
    in_specs = (
        P("loop", "ch"),
        P(None, None, "ch", "loop"),
        P(None, "loop", "ch"),
        P(),
        P(),
        P(None, "ch"),
        P(None, "ch"),
    )
    return jax.shard_map(shards, mesh=mesh, in_specs=in_specs, out_specs=P("loop", "ch"), check_vma=False)
```

```python
import functools

import jax
import jax.numpy as jnp
from jax import lax
from jax.experimental import pallas as pl
from jax.experimental.pallas import tpu as pltpu
from jax.sharding import PartitionSpec as P

MESH = pl.DeviceIdType.MESH
CORES = 2
TILE = 16
PIECES = 2
VMEM_BYTES = 50331648
TO_OUTER = ()
TO_INNER = ((1, 0), (1, 1))
HALVES = 2


def gelu(v):
    return 0.5 * v * (1.0 + jnp.tanh(0.7978845608028654 * (v + 0.044715 * (v * v * v))))


def from_behind(x, axis, by):
    peers = lax.axis_size(axis)
    return lax.ppermute(x, axis, [(i, (i + by) % peers) for i in range(peers)])


def plain_shards(genome, kernel_w, point_w, mid_scale, mid_shift, out_scale, out_shift):
    state = genome
    for b in range(2):
        act = jax.nn.gelu(state.astype(jnp.float32)).astype(jnp.bfloat16)
        before = from_behind(act, "loop", b + 1)
        after = from_behind(act, "loop", -(b + 1))
        kernels = lax.all_gather(kernel_w[b], "loop", axis=2, tiled=True)
        projection = lax.all_gather(point_w[b], "loop", axis=0, tiled=True)
        mid = jnp.dot(before, kernels[0], preferred_element_type=jnp.float32)
        mid = mid + jnp.dot(act, kernels[1], preferred_element_type=jnp.float32)
        mid = mid + jnp.dot(after, kernels[2], preferred_element_type=jnp.float32)
        mid = lax.psum(mid, "ch")
        hid = jax.nn.gelu(mid * mid_scale[b] + mid_shift[b]).astype(jnp.bfloat16)
        proj = jnp.dot(hid, projection, preferred_element_type=jnp.float32)
        state = (state.astype(jnp.float32) + proj * out_scale[b] + out_shift[b]).astype(jnp.bfloat16)
    return state


def kernel(
    peers, xs, x_ref, k_ref, p_ref, ms_ref, mt_ref, osh_ref, oth_ref, o_ref,
    state, act, wbuf, mid, psend, precv, acc, res, cols, coef, os_ref, ot_ref, lmid, lsend, lrecv,
    in_s, in_r, out_s, out_r, wr, wp, wx, wu, wd, wq, we, ys, yr, yls, ylr, loc,
):
    rows, width = x_ref.shape
    part = rows // peers
    slab = p_ref.shape[1]
    zs = peers // (CORES * xs)
    chunk = slab * CORES * xs
    me = lax.axis_index("loop")
    half = lax.axis_index("ch")
    c = lax.rem(me, CORES)
    x = lax.rem(me // CORES, xs)
    z = me // (CORES * xs)
    pad = 2 * part

    def rowset(i):
        return pl.ds(pl.multiple_of(i * part, part), part)

    def a2a_in(to):
        return pltpu.make_async_remote_copy(
            src_ref=x_ref.at[rowset(to)], dst_ref=state.at[rowset(me)],
            send_sem=in_s.at[to], recv_sem=in_r.at[me],
            device_id={"loop": to}, device_id_type=MESH)

    def a2a_in_recv(i):
        frm = lax.rem(me + i, peers)
        return pltpu.make_async_remote_copy(
            src_ref=x_ref.at[rowset(frm)], dst_ref=state.at[rowset(frm)],
            send_sem=in_s.at[frm], recv_sem=in_r.at[frm],
            device_id={"loop": frm}, device_id_type=MESH)

    def a2a_out(to):
        return pltpu.make_async_remote_copy(
            src_ref=res.at[rowset(to)], dst_ref=o_ref.at[rowset(me)],
            send_sem=out_s.at[to], recv_sem=out_r.at[me],
            device_id={"loop": to}, device_id_type=MESH)

    def a2a_out_recv(i):
        frm = lax.rem(me + i, peers)
        return pltpu.make_async_remote_copy(
            src_ref=res.at[rowset(frm)], dst_ref=o_ref.at[rowset(frm)],
            send_sem=out_s.at[frm], recv_sem=out_r.at[frm],
            device_id={"loop": frm}, device_id_type=MESH)

    def plane(s):
        low = jnp.where(z < zs // 2, z, zs - 1 - z)
        at = jnp.where(s <= low, low - s, s)
        return jnp.where(z < zs // 2, at, zs - 1 - at)

    def to_all(copy, prepare=None):
        group = CORES * xs
        spot = lax.rem(me, group)

        @pl.loop(0, zs - 1)
        def _(k):
            base = lax.rem(z + 1 + k, zs) * group
            if prepare is not None:
                prepare(base, group)
            for j in range(group):
                copy(base + lax.rem(spot + j, group)).start()

        if prepare is not None:
            prepare(z * group, group)
        for j in range(1, group):
            copy(z * group + lax.rem(spot + j, group)).start()

    def index(zi, xi, ci):
        return (zi * xs + xi) * CORES + ci

    def place(b, h, owner):
        return wbuf.at[b, pl.ds(h * (4 // PIECES), 4 // PIECES), pl.ds(pl.multiple_of(owner * slab, slab), slab), :]

    def wcopy(b, h, owner, to, sem):
        return pltpu.make_async_remote_copy(
            src_ref=place(b, h, owner),
            dst_ref=place(b, h, owner),
            send_sem=sem, recv_sem=wr.at[b, h, owner],
            device_id={"loop": to}, device_id_type=MESH)

    def got(b, h, owner):
        wcopy(b, h, owner, lax.rem(me + 1, peers), wp.at[b, h, 0]).wait_recv()

    def along(b, h, s, act_on):
        zp = plane(s)
        owner = index(zp, x, c)

        @pl.when((zp <= z) & (z < zs - 1))
        def _():
            act_on(wcopy(b, h, owner, index(lax.rem(z + 1, zs), x, c), wu.at[b, h, s]))

        @pl.when((zp >= z) & (z > 0))
        def _():
            act_on(wcopy(b, h, owner, index(lax.rem(z + zs - 1, zs), x, c), wd.at[b, h, s]))

    edge = jnp.where(z % 2 == 0, z + 1, z - 1)
    outer = (z == 0) | (z == zs - 1)

    def by_edge(b, h, corner):
        return (b, h) in (TO_INNER if corner else TO_OUTER)

    def over_x(b, h, s):
        may = not isinstance(s, int) or s == 1
        skip_outer = may and by_edge(b, h, False)
        skip_inner = may and by_edge(b, h, True)
        keep = z >= 0
        if skip_outer:
            keep = keep & jnp.logical_not(outer & (s == 1))
        if skip_inner:
            keep = keep & (outer | (s != 1))
        return keep

    def across(b, h, s, act_on):
        owner = index(plane(s), x, c)

        @pl.when(over_x(b, h, s))
        def _():
            for j in range(1, xs):
                act_on(wcopy(b, h, owner, index(z, lax.rem(x + j, xs), c), wx.at[b, h, s * (xs - 1) + j - 1]))

        act_on(wcopy(b, h, owner, index(z, x, 1 - c), wp.at[b, h, s]))

    def past_edge(b, h, act_on):
        if not by_edge(b, h, True) and not by_edge(b, h, False):
            return
        copy = wcopy(b, h, index(z, 1 - x, c), index(edge, x, c), we.at[b, h])
        if by_edge(b, h, True):
            @pl.when(outer)
            def _():
                act_on(copy)
        if by_edge(b, h, False):
            @pl.when(jnp.logical_not(outer))
            def _():
                act_on(copy)

    def start(copy):
        copy.start()

    def sent(copy):
        copy.wait_send()

    def forward_column(b, s):
        for h in range(PIECES):
            got(b, h, index(plane(s), x, c))
            along(b, h, s, start)
            across(b, h, s, start)

    def to_partner(b, h, s, j):
        owner = index(plane(s), lax.rem(x + j, xs), c)
        return wcopy(b, h, owner, index(z, x, 1 - c), wq.at[b, h, s * (xs - 1) + j - 1])

    def forward_across(b, s):
        for h in range(PIECES):
            for j in range(1, xs):
                got(b, h, index(plane(s), lax.rem(x + j, xs), c))

                @pl.when(s == 0)
                def _():
                    past_edge(b, h, start)

                to_partner(b, h, s, j).start()

    def arrived(b, s):
        for h in range(PIECES):
            for j in range(xs):
                got(b, h, index(plane(s), j, 1 - c))

    def ycopy(b, s):
        return pltpu.make_async_remote_copy(
            src_ref=psend.at[b, s], dst_ref=precv.at[b, s],
            send_sem=ys.at[b, s], recv_sem=yr.at[b, s],
            device_id={"ch": 1 - half}, device_id_type=MESH)

    def chunk_of(s):
        return pl.ds(pl.multiple_of(plane(s) * chunk, chunk), chunk)

    nt = (((1,), (1,)), ((), ()))
    tn = (((0,), (0,)), ((), ()))

    def middle(b, s):
        at = chunk_of(s)
        shift = (b + 1) * part
        total = None
        for t in range(3):
            term = lax.dot_general(
                wbuf[b, t, at, :], act[pl.ds(pad + (t - 1) * shift, rows), :], nt,
                preferred_element_type=jnp.float32)
            total = term if total is None else total + term
        mid[s] = total
        psend[b, s] = total.astype(jnp.bfloat16)
        ycopy(b, s).start()

    def project(b, s):
        at = chunk_of(s)
        ycopy(b, s).wait_recv()
        total = mid[s] + precv[b, s].astype(jnp.float32)
        hid = gelu(total * cols[at, pl.ds(b, 1)] + cols[at, pl.ds(2 + b, 1)]).astype(jnp.bfloat16)
        acc[...] += lax.dot_general(hid, wbuf[b, 3, at, :], tn, preferred_element_type=jnp.float32)

    step = 64 if rows % 64 == 0 else part

    def activate(src):
        @pl.loop(0, rows // step)
        def _(i):
            at = pl.ds(pl.multiple_of(i * step, step), step)
            act[pl.ds(pl.multiple_of(pad + i * step, part), step), :] = gelu(
                src[at, :].astype(jnp.float32)).astype(jnp.bfloat16)

        act[pl.ds(0, pad), :] = act[pl.ds(rows, pad), :]
        act[pl.ds(pad + rows, pad), :] = act[pl.ds(pad, pad), :]

    def update(b, src, dst):
        @pl.loop(0, rows // step)
        def _(i):
            at = pl.ds(pl.multiple_of(i * step, step), step)
            dst[at, :] = (
                src[at, :].astype(jnp.float32)
                + acc[at, :] * os_ref[pl.ds(b, 1), :] + ot_ref[pl.ds(b, 1), :]
            ).astype(jnp.bfloat16)

    def finish(first, count):
        at = pl.ds(pl.multiple_of(first * part, part), count * part)
        res[at, :] = (
            state[at, :].astype(jnp.float32) + acc[at, :] * os_ref[pl.ds(1, 1), :] + ot_ref[pl.ds(1, 1), :]
        ).astype(jnp.bfloat16)

    own_x = pltpu.make_async_copy(x_ref.at[rowset(me)], state.at[rowset(me)], loc.at[0])
    own_w = []
    for b in range(2):
        at = pl.ds(pl.multiple_of(me * slab, slab), slab)
        own_w.append(pltpu.make_async_copy(k_ref.at[b], wbuf.at[b, pl.ds(0, 3), at, :], loc.at[1 + 2 * b]))
        own_w.append(pltpu.make_async_copy(p_ref.at[b], wbuf.at[b, 3, at, :], loc.at[2 + 2 * b]))

    barrier = pltpu.get_barrier_semaphore()

    @pl.loop(1, peers)
    def _(i):
        pl.semaphore_signal(barrier, inc=1, device_id={"loop": lax.rem(me + i, peers)}, device_id_type=MESH)

    pl.semaphore_signal(barrier, inc=1, device_id={"ch": 1 - half}, device_id_type=MESH)
    for copy in own_w:
        copy.start()
    own_x.start()
    coef[...] = jnp.zeros_like(coef)
    small = [
        pltpu.make_async_copy(ms_ref, coef.at[pl.ds(0, 2)], loc.at[5]),
        pltpu.make_async_copy(mt_ref, coef.at[pl.ds(2, 2)], loc.at[6]),
        pltpu.make_async_copy(osh_ref, os_ref, loc.at[7]),
        pltpu.make_async_copy(oth_ref, ot_ref, loc.at[8]),
    ]
    for copy in small:
        copy.start()
    acc[...] = jnp.zeros_like(acc)
    for copy in own_w:
        copy.wait()
    own_x.wait()
    for copy in small:
        copy.wait()
    cols[...] = coef[...].T
    pl.semaphore_wait(barrier, peers)

    def own_slab(b):
        for h in range(PIECES):
            along(b, h, 0, start)
            across(b, h, 0, start)

    inner = jnp.logical_not(outer)

    own_slab(0)
    to_all(a2a_in)
    forward_column(0, 1)

    @pl.when(inner)
    def _():
        forward_column(0, 2)

    @pl.loop(1, peers)
    def _(i):
        a2a_in_recv(i).wait_recv()

    for h in range(PIECES):
        across(1, h, 0, start)

        @pl.when(outer)
        def _():
            along(1, h, 0, start)

    activate(state)

    @pl.loop(0, zs + 1)
    def _(s):
        @pl.when(s < zs)
        def _():
            forward_across(0, s)
            arrived(0, s)
            middle(0, s)

        @pl.when(outer & (s == 0))
        def _():
            forward_column(0, 2)

        @pl.when(inner & (s == 0))
        def _():
            along(1, 0, 0, start)

        @pl.when((outer & (s == 1)) | (inner & (s == 0)))
        def _():
            forward_column(0, 3)

        @pl.when(inner & (s == 0))
        def _():
            along(1, 1, 0, start)

        @pl.when((outer & (s == 2)) | (inner & (s == 1)))
        def _():
            forward_across(1, 0)
            forward_column(1, 1)

        @pl.when((outer & (s == 3)) | (inner & (s == 2)))
        def _():
            forward_column(1, 2)

        @pl.when(inner & (s == 3))
        def _():
            forward_column(1, 3)

        @pl.when(s > 0)
        def _():
            project(0, s - 1)

    update(0, state, state)
    activate(state)
    acc[...] = jnp.zeros_like(acc)

    last = zs - 1

    @pl.loop(0, last)
    def _(s):
        @pl.when(s > 0)
        def _():
            forward_across(1, s)

        arrived(1, s)
        middle(1, s)

        @pl.when(outer & (s == 1))
        def _():
            forward_column(1, 3)

    @pl.loop(0, last - 1)
    def _(s):
        project(1, s)

    forward_across(1, last)
    arrived(1, last)
    group = CORES * xs
    level = group * part
    far = jnp.where(z < zs // 2, 1, 0)
    span = rows // HALVES
    last_at = chunk_of(last)
    shift = 2 * part

    def halfset(q):
        return pl.ds(pl.multiple_of(q * span, span), span)

    def lcopy(k):
        return pltpu.make_async_remote_copy(
            src_ref=lsend.at[k], dst_ref=lrecv.at[k],
            send_sem=yls.at[k], recv_sem=ylr.at[k],
            device_id={"ch": 1 - half}, device_id_type=MESH)

    def to_half(k):
        return jnp.where(far == 1, 1 - k, k) if HALVES == 2 else k

    for k in range(HALVES):
        q = to_half(k)
        total = None
        for t in range(3):
            term = lax.dot_general(
                wbuf[1, t, last_at, :],
                act[pl.ds(pl.multiple_of(pad + (t - 1) * shift + q * span, part), span), :], nt,
                preferred_element_type=jnp.float32)
            total = term if total is None else total + term
        lmid[k] = total
        lsend[k] = total.astype(jnp.bfloat16)
        lcopy(k).start()

    project(1, last - 1)

    for k in range(HALVES):
        q = to_half(k)
        lcopy(k).wait_recv()
        total = lmid[k] + lrecv[k].astype(jnp.float32)
        hid = gelu(total * cols[last_at, pl.ds(1, 1)] + cols[last_at, pl.ds(3, 1)]).astype(jnp.bfloat16)
        acc[halfset(q), :] += lax.dot_general(hid, wbuf[1, 3, last_at, :], tn, preferred_element_type=jnp.float32)

        def send_level(zt):
            finish(zt * group, group)
            spot = lax.rem(me, group)
            for j in range(group):
                to = zt * group + lax.rem(spot + j, group)

                @pl.when(to != me)
                def _():
                    a2a_out(to).start()

        per = zs // HALVES

        @pl.loop(0, per)
        def _(i):
            at = jnp.where(z < zs // 2, per - 1 - i, i)
            send_level(q * per + at)

    own_o = pltpu.make_async_copy(res.at[rowset(me)], o_ref.at[rowset(me)], loc.at[0])
    own_o.start()
    own_o.wait()

    @pl.loop(1, peers)
    def _(i):
        a2a_out_recv(i).wait_recv()

    for b in range(2):
        for h in range(PIECES):
            along(b, h, 0, sent)
            across(b, h, 0, sent)
            past_edge(b, h, sent)

        @pl.loop(0, zs)
        def _(s):
            for h in range(PIECES):
                @pl.when(s > 0)
                def _():
                    along(b, h, s, sent)
                    across(b, h, s, sent)

                for j in range(1, xs):
                    to_partner(b, h, s, j).wait_send()

            @pl.when((s < zs - 1) | (b == 0))
            def _():
                ycopy(b, s).wait_send()

    for k in range(HALVES):
        lcopy(k).wait_send()

    @pl.loop(1, peers)
    def _(i):
        a2a_in(lax.rem(me + i, peers)).wait_send()
        a2a_out(lax.rem(me + i, peers)).wait_send()


def fused_shards(genome, kernel_w, point_w, mid_scale, mid_shift, out_scale, out_shift):
    peers = lax.axis_size("loop")
    rows, width = genome.shape
    slab = point_w.shape[1]
    mids = mid_scale.shape[1]
    xs = 2
    zs = peers // (CORES * xs)
    chunk = slab * CORES * xs
    part = rows // peers
    bf16, f32 = jnp.bfloat16, jnp.float32
    dma = pltpu.SemaphoreType.DMA
    hbm = pl.BlockSpec(memory_space=pltpu.HBM)
    vmem = pl.BlockSpec(memory_space=pltpu.VMEM)
    operands = (genome, jnp.swapaxes(kernel_w, 2, 3), point_w, mid_scale, mid_shift, out_scale, out_shift)
    return pl.pallas_call(
        functools.partial(kernel, peers, xs),
        out_shape=jax.ShapeDtypeStruct((rows, width), bf16),
        in_specs=[hbm] * len(operands),
        out_specs=vmem,
        scratch_shapes=[
            pltpu.VMEM((rows, width), bf16),
            pltpu.VMEM((rows + 4 * part, width), bf16),
            pltpu.VMEM((2, 4, mids, width), bf16),
            pltpu.VMEM((zs, chunk, rows), f32),
            pltpu.VMEM((2, zs, chunk, rows), bf16),
            pltpu.VMEM((2, zs, chunk, rows), bf16),
            pltpu.VMEM((rows, width), f32),
            pltpu.VMEM((rows, width), bf16),
            pltpu.VMEM((mids, 8), f32),
            pltpu.VMEM((8, mids), f32),
            pltpu.VMEM((2, width), f32),
            pltpu.VMEM((2, width), f32),
            pltpu.VMEM((HALVES, chunk, rows // HALVES), f32),
            pltpu.VMEM((HALVES, chunk, rows // HALVES), bf16),
            pltpu.VMEM((HALVES, chunk, rows // HALVES), bf16),
            dma((peers,)), dma((peers,)), dma((peers,)), dma((peers,)),
            dma((2, PIECES, peers)), dma((2, PIECES, zs)), dma((2, PIECES, zs * (xs - 1))),
            dma((2, PIECES, zs)), dma((2, PIECES, zs)), dma((2, PIECES, zs * (xs - 1))),
            dma((2, PIECES)), dma((2, zs)), dma((2, zs)), dma((HALVES,)), dma((HALVES,)), dma((9,)),
        ],
        compiler_params=pltpu.CompilerParams(
            collective_id=0, has_side_effects=True, vmem_limit_bytes=VMEM_BYTES),
    )(*(pltpu.with_memory_space_constraint(a, pltpu.HBM) for a in operands))


def shards(genome, kernel_w, *rest):
    peers = lax.axis_size("loop")
    rows, width = genome.shape
    slab = kernel_w.shape[3]
    fits = (
        peers == CORES * 2 * 4 and rows % (peers * TILE) == 0 and slab % TILE == 0
        and width % 128 == 0 and rows % 128 == 0 and lax.axis_size("ch") == 2
    )
    return (fused_shards if fits else plain_shards)(genome, kernel_w, *rest)


def solution(mesh):
    in_specs = (
        P("loop", "ch"),
        P(None, None, "ch", "loop"),
        P(None, "loop", "ch"),
        P(),
        P(),
        P(None, "ch"),
        P(None, "ch"),
    )
    return jax.shard_map(shards, mesh=mesh, in_specs=in_specs, out_specs=P("loop", "ch"), check_vma=False)
```

```python
import functools

import jax
import jax.numpy as jnp
from jax import lax
from jax.experimental import pallas as pl
from jax.experimental.pallas import tpu as pltpu
from jax.sharding import PartitionSpec as P

MESH = pl.DeviceIdType.MESH
CORES = 2
TILE = 16
PIECES = 2
VMEM_BYTES = 50331648
TO_OUTER = ()
TO_INNER = ((0, 0), (0, 1), (1, 0), (1, 1))
HALVES = 2


def gelu(v):
    return 0.5 * v * (1.0 + jnp.tanh(0.7978845608028654 * (v + 0.044715 * (v * v * v))))


def from_behind(x, axis, by):
    peers = lax.axis_size(axis)
    return lax.ppermute(x, axis, [(i, (i + by) % peers) for i in range(peers)])


def plain_shards(genome, kernel_w, point_w, mid_scale, mid_shift, out_scale, out_shift):
    state = genome
    for b in range(2):
        act = jax.nn.gelu(state.astype(jnp.float32)).astype(jnp.bfloat16)
        before = from_behind(act, "loop", b + 1)
        after = from_behind(act, "loop", -(b + 1))
        kernels = lax.all_gather(kernel_w[b], "loop", axis=2, tiled=True)
        projection = lax.all_gather(point_w[b], "loop", axis=0, tiled=True)
        mid = jnp.dot(before, kernels[0], preferred_element_type=jnp.float32)
        mid = mid + jnp.dot(act, kernels[1], preferred_element_type=jnp.float32)
        mid = mid + jnp.dot(after, kernels[2], preferred_element_type=jnp.float32)
        mid = lax.psum(mid, "ch")
        hid = jax.nn.gelu(mid * mid_scale[b] + mid_shift[b]).astype(jnp.bfloat16)
        proj = jnp.dot(hid, projection, preferred_element_type=jnp.float32)
        state = (state.astype(jnp.float32) + proj * out_scale[b] + out_shift[b]).astype(jnp.bfloat16)
    return state


def kernel(
    peers, xs, x_ref, k_ref, p_ref, ms_ref, mt_ref, osh_ref, oth_ref, o_ref,
    state, act, wbuf, mid, psend, precv, acc, res, cols, coef, os_ref, ot_ref, lmid, lsend, lrecv,
    in_s, in_r, out_s, out_r, wr, wp, wx, wu, wd, wq, we, ys, yr, yls, ylr, loc,
):
    rows, width = x_ref.shape
    part = rows // peers
    slab = p_ref.shape[1]
    zs = peers // (CORES * xs)
    chunk = slab * CORES * xs
    me = lax.axis_index("loop")
    half = lax.axis_index("ch")
    c = lax.rem(me, CORES)
    x = lax.rem(me // CORES, xs)
    z = me // (CORES * xs)
    pad = 2 * part

    def rowset(i):
        return pl.ds(pl.multiple_of(i * part, part), part)

    def a2a_in(to):
        return pltpu.make_async_remote_copy(
            src_ref=x_ref.at[rowset(to)], dst_ref=state.at[rowset(me)],
            send_sem=in_s.at[to], recv_sem=in_r.at[me],
            device_id={"loop": to}, device_id_type=MESH)

    def a2a_in_recv(i):
        frm = lax.rem(me + i, peers)
        return pltpu.make_async_remote_copy(
            src_ref=x_ref.at[rowset(frm)], dst_ref=state.at[rowset(frm)],
            send_sem=in_s.at[frm], recv_sem=in_r.at[frm],
            device_id={"loop": frm}, device_id_type=MESH)

    def a2a_out(to):
        return pltpu.make_async_remote_copy(
            src_ref=res.at[rowset(to)], dst_ref=o_ref.at[rowset(me)],
            send_sem=out_s.at[to], recv_sem=out_r.at[me],
            device_id={"loop": to}, device_id_type=MESH)

    def a2a_out_recv(i):
        frm = lax.rem(me + i, peers)
        return pltpu.make_async_remote_copy(
            src_ref=res.at[rowset(frm)], dst_ref=o_ref.at[rowset(frm)],
            send_sem=out_s.at[frm], recv_sem=out_r.at[frm],
            device_id={"loop": frm}, device_id_type=MESH)

    def plane(s):
        low = jnp.where(z < zs // 2, z, zs - 1 - z)
        at = jnp.where(s <= low, low - s, s)
        return jnp.where(z < zs // 2, at, zs - 1 - at)

    def to_all(copy, prepare=None):
        group = CORES * xs
        spot = lax.rem(me, group)

        @pl.loop(0, zs - 1)
        def _(k):
            base = lax.rem(z + 1 + k, zs) * group
            if prepare is not None:
                prepare(base, group)
            for j in range(group):
                copy(base + lax.rem(spot + j, group)).start()

        if prepare is not None:
            prepare(z * group, group)
        for j in range(1, group):
            copy(z * group + lax.rem(spot + j, group)).start()

    def index(zi, xi, ci):
        return (zi * xs + xi) * CORES + ci

    def place(b, h, owner):
        return wbuf.at[b, pl.ds(h * (4 // PIECES), 4 // PIECES), pl.ds(pl.multiple_of(owner * slab, slab), slab), :]

    def wcopy(b, h, owner, to, sem):
        return pltpu.make_async_remote_copy(
            src_ref=place(b, h, owner),
            dst_ref=place(b, h, owner),
            send_sem=sem, recv_sem=wr.at[b, h, owner],
            device_id={"loop": to}, device_id_type=MESH)

    def got(b, h, owner):
        wcopy(b, h, owner, lax.rem(me + 1, peers), wp.at[b, h, 0]).wait_recv()

    def along(b, h, s, act_on):
        zp = plane(s)
        owner = index(zp, x, c)

        @pl.when((zp <= z) & (z < zs - 1))
        def _():
            act_on(wcopy(b, h, owner, index(lax.rem(z + 1, zs), x, c), wu.at[b, h, s]))

        @pl.when((zp >= z) & (z > 0))
        def _():
            act_on(wcopy(b, h, owner, index(lax.rem(z + zs - 1, zs), x, c), wd.at[b, h, s]))

    edge = jnp.where(z % 2 == 0, z + 1, z - 1)
    outer = (z == 0) | (z == zs - 1)

    def by_edge(b, h, corner):
        return (b, h) in (TO_INNER if corner else TO_OUTER)

    def over_x(b, h, s):
        may = not isinstance(s, int) or s == 1
        skip_outer = may and by_edge(b, h, False)
        skip_inner = may and by_edge(b, h, True)
        keep = z >= 0
        if skip_outer:
            keep = keep & jnp.logical_not(outer & (s == 1))
        if skip_inner:
            keep = keep & (outer | (s != 1))
        return keep

    def across(b, h, s, act_on):
        owner = index(plane(s), x, c)

        @pl.when(over_x(b, h, s))
        def _():
            for j in range(1, xs):
                act_on(wcopy(b, h, owner, index(z, lax.rem(x + j, xs), c), wx.at[b, h, s * (xs - 1) + j - 1]))

        act_on(wcopy(b, h, owner, index(z, x, 1 - c), wp.at[b, h, s]))

    def past_edge(b, h, act_on):
        if not by_edge(b, h, True) and not by_edge(b, h, False):
            return
        copy = wcopy(b, h, index(z, 1 - x, c), index(edge, x, c), we.at[b, h])
        if by_edge(b, h, True):
            @pl.when(outer)
            def _():
                act_on(copy)
        if by_edge(b, h, False):
            @pl.when(jnp.logical_not(outer))
            def _():
                act_on(copy)

    def start(copy):
        copy.start()

    def sent(copy):
        copy.wait_send()

    def forward_column(b, s):
        for h in range(PIECES):
            got(b, h, index(plane(s), x, c))
            along(b, h, s, start)
            across(b, h, s, start)

    def to_partner(b, h, s, j):
        owner = index(plane(s), lax.rem(x + j, xs), c)
        return wcopy(b, h, owner, index(z, x, 1 - c), wq.at[b, h, s * (xs - 1) + j - 1])

    def forward_across(b, s):
        for h in range(PIECES):
            for j in range(1, xs):
                got(b, h, index(plane(s), lax.rem(x + j, xs), c))

                @pl.when(s == 0)
                def _():
                    past_edge(b, h, start)

                to_partner(b, h, s, j).start()

    def arrived(b, s):
        for h in range(PIECES):
            for j in range(xs):
                got(b, h, index(plane(s), j, 1 - c))

    def ycopy(b, s):
        return pltpu.make_async_remote_copy(
            src_ref=psend.at[b, s], dst_ref=precv.at[b, s],
            send_sem=ys.at[b, s], recv_sem=yr.at[b, s],
            device_id={"ch": 1 - half}, device_id_type=MESH)

    def chunk_of(s):
        return pl.ds(pl.multiple_of(plane(s) * chunk, chunk), chunk)

    nt = (((1,), (1,)), ((), ()))
    tn = (((0,), (0,)), ((), ()))

    def middle(b, s):
        at = chunk_of(s)
        shift = (b + 1) * part
        total = None
        for t in range(3):
            term = lax.dot_general(
                wbuf[b, t, at, :], act[pl.ds(pad + (t - 1) * shift, rows), :], nt,
                preferred_element_type=jnp.float32)
            total = term if total is None else total + term
        mid[s] = total
        psend[b, s] = total.astype(jnp.bfloat16)
        ycopy(b, s).start()

    def project(b, s):
        at = chunk_of(s)
        ycopy(b, s).wait_recv()
        total = mid[s] + precv[b, s].astype(jnp.float32)
        hid = gelu(total * cols[at, pl.ds(b, 1)] + cols[at, pl.ds(2 + b, 1)]).astype(jnp.bfloat16)
        acc[...] += lax.dot_general(hid, wbuf[b, 3, at, :], tn, preferred_element_type=jnp.float32)

    step = 64 if rows % 64 == 0 else part

    def activate(src):
        @pl.loop(0, rows // step)
        def _(i):
            at = pl.ds(pl.multiple_of(i * step, step), step)
            act[pl.ds(pl.multiple_of(pad + i * step, part), step), :] = gelu(
                src[at, :].astype(jnp.float32)).astype(jnp.bfloat16)

        act[pl.ds(0, pad), :] = act[pl.ds(rows, pad), :]
        act[pl.ds(pad + rows, pad), :] = act[pl.ds(pad, pad), :]

    def update(b, src, dst):
        @pl.loop(0, rows // step)
        def _(i):
            at = pl.ds(pl.multiple_of(i * step, step), step)
            dst[at, :] = (
                src[at, :].astype(jnp.float32)
                + acc[at, :] * os_ref[pl.ds(b, 1), :] + ot_ref[pl.ds(b, 1), :]
            ).astype(jnp.bfloat16)

    def finish(first, count):
        at = pl.ds(pl.multiple_of(first * part, part), count * part)
        res[at, :] = (
            state[at, :].astype(jnp.float32) + acc[at, :] * os_ref[pl.ds(1, 1), :] + ot_ref[pl.ds(1, 1), :]
        ).astype(jnp.bfloat16)

    own_x = pltpu.make_async_copy(x_ref.at[rowset(me)], state.at[rowset(me)], loc.at[0])
    own_w = []
    for b in range(2):
        at = pl.ds(pl.multiple_of(me * slab, slab), slab)
        own_w.append(pltpu.make_async_copy(k_ref.at[b], wbuf.at[b, pl.ds(0, 3), at, :], loc.at[1 + 2 * b]))
        own_w.append(pltpu.make_async_copy(p_ref.at[b], wbuf.at[b, 3, at, :], loc.at[2 + 2 * b]))

    barrier = pltpu.get_barrier_semaphore()

    @pl.loop(1, peers)
    def _(i):
        pl.semaphore_signal(barrier, inc=1, device_id={"loop": lax.rem(me + i, peers)}, device_id_type=MESH)

    pl.semaphore_signal(barrier, inc=1, device_id={"ch": 1 - half}, device_id_type=MESH)
    for copy in own_w:
        copy.start()
    own_x.start()
    coef[...] = jnp.zeros_like(coef)
    small = [
        pltpu.make_async_copy(ms_ref, coef.at[pl.ds(0, 2)], loc.at[5]),
        pltpu.make_async_copy(mt_ref, coef.at[pl.ds(2, 2)], loc.at[6]),
        pltpu.make_async_copy(osh_ref, os_ref, loc.at[7]),
        pltpu.make_async_copy(oth_ref, ot_ref, loc.at[8]),
    ]
    for copy in small:
        copy.start()
    acc[...] = jnp.zeros_like(acc)
    for copy in own_w:
        copy.wait()
    own_x.wait()
    for copy in small:
        copy.wait()
    cols[...] = coef[...].T
    pl.semaphore_wait(barrier, peers)

    def own_slab(b):
        for h in range(PIECES):
            along(b, h, 0, start)
            across(b, h, 0, start)

    inner = jnp.logical_not(outer)

    own_slab(0)
    to_all(a2a_in)
    for h in range(PIECES):
        across(1, h, 0, start)

        @pl.when(outer)
        def _():
            along(1, h, 0, start)

    forward_column(0, 1)

    @pl.when(inner)
    def _():
        forward_column(0, 2)

    forward_across(0, 0)

    @pl.loop(1, peers)
    def _(i):
        a2a_in_recv(i).wait_recv()

    activate(state)

    @pl.loop(0, zs + 1)
    def _(s):
        @pl.when(s < zs)
        def _():
            @pl.when(s > 0)
            def _():
                forward_across(0, s)

            arrived(0, s)
            middle(0, s)

        @pl.when(outer & (s == 0))
        def _():
            forward_column(0, 2)

        @pl.when(inner & (s == 0))
        def _():
            along(1, 0, 0, start)

        @pl.when((outer & (s == 1)) | (inner & (s == 0)))
        def _():
            forward_column(0, 3)

        @pl.when(inner & (s == 0))
        def _():
            along(1, 1, 0, start)

        @pl.when((outer & (s == 2)) | (inner & (s == 1)))
        def _():
            forward_across(1, 0)
            forward_column(1, 1)

        @pl.when(inner & (s == 2))
        def _():
            forward_column(1, 2)

        @pl.when(inner & (s == 3))
        def _():
            forward_column(1, 3)

        @pl.when(s > 0)
        def _():
            project(0, s - 1)

        @pl.when(outer & (s == 3))
        def _():
            forward_column(1, 2)

    update(0, state, state)
    activate(state)
    acc[...] = jnp.zeros_like(acc)

    last = zs - 1

    @pl.loop(0, last)
    def _(s):
        @pl.when(s > 0)
        def _():
            forward_across(1, s)

        arrived(1, s)
        middle(1, s)

        @pl.when(outer & (s == 1))
        def _():
            forward_column(1, 3)

    project(1, 0)

    forward_across(1, last)
    arrived(1, last)
    group = CORES * xs
    level = group * part
    far = jnp.where(z < zs // 2, 1, 0)
    span = rows // HALVES
    last_at = chunk_of(last)
    shift = 2 * part

    def halfset(q):
        return pl.ds(pl.multiple_of(q * span, span), span)

    def lcopy(k):
        return pltpu.make_async_remote_copy(
            src_ref=lsend.at[k], dst_ref=lrecv.at[k],
            send_sem=yls.at[k], recv_sem=ylr.at[k],
            device_id={"ch": 1 - half}, device_id_type=MESH)

    def to_half(k):
        return jnp.where(far == 1, 1 - k, k) if HALVES == 2 else k

    for k in range(HALVES):
        q = to_half(k)
        total = None
        for t in range(3):
            term = lax.dot_general(
                wbuf[1, t, last_at, :],
                act[pl.ds(pl.multiple_of(pad + (t - 1) * shift + q * span, part), span), :], nt,
                preferred_element_type=jnp.float32)
            total = term if total is None else total + term
        lmid[k] = total
        lsend[k] = total.astype(jnp.bfloat16)
        if k == 0:
            lcopy(k).start()

    project(1, last - 2)
    project(1, last - 1)
    lcopy(1).start()

    for k in range(HALVES):
        q = to_half(k)
        lcopy(k).wait_recv()
        total = lmid[k] + lrecv[k].astype(jnp.float32)
        hid = gelu(total * cols[last_at, pl.ds(1, 1)] + cols[last_at, pl.ds(3, 1)]).astype(jnp.bfloat16)
        acc[halfset(q), :] += lax.dot_general(hid, wbuf[1, 3, last_at, :], tn, preferred_element_type=jnp.float32)

        def send_level(zt):
            finish(zt * group, group)
            spot = lax.rem(me, group)
            for j in range(group):
                to = zt * group + lax.rem(spot + j, group)

                @pl.when(to != me)
                def _():
                    a2a_out(to).start()

        per = zs // HALVES

        @pl.loop(0, per)
        def _(i):
            at = jnp.where(z < zs // 2, per - 1 - i, i)
            send_level(q * per + at)

    own_o = pltpu.make_async_copy(res.at[rowset(me)], o_ref.at[rowset(me)], loc.at[0])
    own_o.start()
    own_o.wait()

    @pl.loop(1, peers)
    def _(i):
        a2a_out_recv(i).wait_recv()

    for b in range(2):
        for h in range(PIECES):
            along(b, h, 0, sent)
            across(b, h, 0, sent)
            past_edge(b, h, sent)

        @pl.loop(0, zs)
        def _(s):
            for h in range(PIECES):
                @pl.when(s > 0)
                def _():
                    along(b, h, s, sent)
                    across(b, h, s, sent)

                for j in range(1, xs):
                    to_partner(b, h, s, j).wait_send()

            @pl.when((s < zs - 1) | (b == 0))
            def _():
                ycopy(b, s).wait_send()

    for k in range(HALVES):
        lcopy(k).wait_send()

    @pl.loop(1, peers)
    def _(i):
        a2a_in(lax.rem(me + i, peers)).wait_send()
        a2a_out(lax.rem(me + i, peers)).wait_send()


def fused_shards(genome, kernel_w, point_w, mid_scale, mid_shift, out_scale, out_shift):
    peers = lax.axis_size("loop")
    rows, width = genome.shape
    slab = point_w.shape[1]
    mids = mid_scale.shape[1]
    xs = 2
    zs = peers // (CORES * xs)
    chunk = slab * CORES * xs
    part = rows // peers
    bf16, f32 = jnp.bfloat16, jnp.float32
    dma = pltpu.SemaphoreType.DMA
    hbm = pl.BlockSpec(memory_space=pltpu.HBM)
    vmem = pl.BlockSpec(memory_space=pltpu.VMEM)
    operands = (genome, jnp.swapaxes(kernel_w, 2, 3), point_w, mid_scale, mid_shift, out_scale, out_shift)
    return pl.pallas_call(
        functools.partial(kernel, peers, xs),
        out_shape=jax.ShapeDtypeStruct((rows, width), bf16),
        in_specs=[hbm] * len(operands),
        out_specs=vmem,
        scratch_shapes=[
            pltpu.VMEM((rows, width), bf16),
            pltpu.VMEM((rows + 4 * part, width), bf16),
            pltpu.VMEM((2, 4, mids, width), bf16),
            pltpu.VMEM((zs, chunk, rows), f32),
            pltpu.VMEM((2, zs, chunk, rows), bf16),
            pltpu.VMEM((2, zs, chunk, rows), bf16),
            pltpu.VMEM((rows, width), f32),
            pltpu.VMEM((rows, width), bf16),
            pltpu.VMEM((mids, 8), f32),
            pltpu.VMEM((8, mids), f32),
            pltpu.VMEM((2, width), f32),
            pltpu.VMEM((2, width), f32),
            pltpu.VMEM((HALVES, chunk, rows // HALVES), f32),
            pltpu.VMEM((HALVES, chunk, rows // HALVES), bf16),
            pltpu.VMEM((HALVES, chunk, rows // HALVES), bf16),
            dma((peers,)), dma((peers,)), dma((peers,)), dma((peers,)),
            dma((2, PIECES, peers)), dma((2, PIECES, zs)), dma((2, PIECES, zs * (xs - 1))),
            dma((2, PIECES, zs)), dma((2, PIECES, zs)), dma((2, PIECES, zs * (xs - 1))),
            dma((2, PIECES)), dma((2, zs)), dma((2, zs)), dma((HALVES,)), dma((HALVES,)), dma((9,)),
        ],
        compiler_params=pltpu.CompilerParams(
            collective_id=0, has_side_effects=True, vmem_limit_bytes=VMEM_BYTES),
    )(*(pltpu.with_memory_space_constraint(a, pltpu.HBM) for a in operands))


def shards(genome, kernel_w, *rest):
    peers = lax.axis_size("loop")
    rows, width = genome.shape
    slab = kernel_w.shape[3]
    fits = (
        peers == CORES * 2 * 4 and rows % (peers * TILE) == 0 and slab % TILE == 0
        and width % 128 == 0 and rows % 128 == 0 and lax.axis_size("ch") == 2
    )
    return (fused_shards if fits else plain_shards)(genome, kernel_w, *rest)


def solution(mesh):
    in_specs = (
        P("loop", "ch"),
        P(None, None, "ch", "loop"),
        P(None, "loop", "ch"),
        P(),
        P(),
        P(None, "ch"),
        P(None, "ch"),
    )
    return jax.shard_map(shards, mesh=mesh, in_specs=in_specs, out_specs=P("loop", "ch"), check_vma=False)
```

```python
import functools

import jax
import jax.numpy as jnp
from jax import lax
from jax.experimental import pallas as pl
from jax.experimental.pallas import tpu as pltpu
from jax.sharding import PartitionSpec as P

MESH = pl.DeviceIdType.MESH
CORES = 2
TILE = 16
PIECES = 2
VMEM_BYTES = 50331648
TO_OUTER = ()
TO_INNER = ((0, 0), (0, 1), (1, 0), (1, 1))
HALVES = 2


def gelu(v):
    return 0.5 * v * (1.0 + jnp.tanh(0.7978845608028654 * (v + 0.044715 * (v * v * v))))


def from_behind(x, axis, by):
    peers = lax.axis_size(axis)
    return lax.ppermute(x, axis, [(i, (i + by) % peers) for i in range(peers)])


def plain_shards(genome, kernel_w, point_w, mid_scale, mid_shift, out_scale, out_shift):
    state = genome
    for b in range(2):
        act = jax.nn.gelu(state.astype(jnp.float32)).astype(jnp.bfloat16)
        before = from_behind(act, "loop", b + 1)
        after = from_behind(act, "loop", -(b + 1))
        kernels = lax.all_gather(kernel_w[b], "loop", axis=2, tiled=True)
        projection = lax.all_gather(point_w[b], "loop", axis=0, tiled=True)
        mid = jnp.dot(before, kernels[0], preferred_element_type=jnp.float32)
        mid = mid + jnp.dot(act, kernels[1], preferred_element_type=jnp.float32)
        mid = mid + jnp.dot(after, kernels[2], preferred_element_type=jnp.float32)
        mid = lax.psum(mid, "ch")
        hid = jax.nn.gelu(mid * mid_scale[b] + mid_shift[b]).astype(jnp.bfloat16)
        proj = jnp.dot(hid, projection, preferred_element_type=jnp.float32)
        state = (state.astype(jnp.float32) + proj * out_scale[b] + out_shift[b]).astype(jnp.bfloat16)
    return state


def kernel(
    peers, xs, x_ref, k_ref, p_ref, ms_ref, mt_ref, osh_ref, oth_ref, o_ref,
    state, act, wbuf, mid, psend, precv, acc, res, cols, coef, os_ref, ot_ref, lmid, lsend, lrecv,
    in_s, in_r, out_s, out_r, wr, wp, wx, wu, wd, wq, we, ys, yr, yls, ylr, loc,
):
    rows, width = x_ref.shape
    part = rows // peers
    slab = p_ref.shape[1]
    zs = peers // (CORES * xs)
    chunk = slab * CORES * xs
    me = lax.axis_index("loop")
    half = lax.axis_index("ch")
    c = lax.rem(me, CORES)
    x = lax.rem(me // CORES, xs)
    z = me // (CORES * xs)
    pad = 2 * part

    def rowset(i):
        return pl.ds(pl.multiple_of(i * part, part), part)

    def a2a_in(to):
        return pltpu.make_async_remote_copy(
            src_ref=x_ref.at[rowset(to)], dst_ref=state.at[rowset(me)],
            send_sem=in_s.at[to], recv_sem=in_r.at[me],
            device_id={"loop": to}, device_id_type=MESH)

    def a2a_in_recv(i):
        frm = lax.rem(me + i, peers)
        return pltpu.make_async_remote_copy(
            src_ref=x_ref.at[rowset(frm)], dst_ref=state.at[rowset(frm)],
            send_sem=in_s.at[frm], recv_sem=in_r.at[frm],
            device_id={"loop": frm}, device_id_type=MESH)

    def a2a_out(to):
        return pltpu.make_async_remote_copy(
            src_ref=res.at[rowset(to)], dst_ref=o_ref.at[rowset(me)],
            send_sem=out_s.at[to], recv_sem=out_r.at[me],
            device_id={"loop": to}, device_id_type=MESH)

    def a2a_out_recv(i):
        frm = lax.rem(me + i, peers)
        return pltpu.make_async_remote_copy(
            src_ref=res.at[rowset(frm)], dst_ref=o_ref.at[rowset(frm)],
            send_sem=out_s.at[frm], recv_sem=out_r.at[frm],
            device_id={"loop": frm}, device_id_type=MESH)

    def plane(s):
        low = jnp.where(z < zs // 2, z, zs - 1 - z)
        at = jnp.where(s <= low, low - s, s)
        return jnp.where(z < zs // 2, at, zs - 1 - at)

    def to_all(copy, prepare=None):
        group = CORES * xs
        spot = lax.rem(me, group)

        @pl.loop(0, zs - 1)
        def _(k):
            base = lax.rem(z + 1 + k, zs) * group
            if prepare is not None:
                prepare(base, group)
            for j in range(group):
                copy(base + lax.rem(spot + j, group)).start()

        if prepare is not None:
            prepare(z * group, group)
        for j in range(1, group):
            copy(z * group + lax.rem(spot + j, group)).start()

    def index(zi, xi, ci):
        return (zi * xs + xi) * CORES + ci

    def place(b, h, owner):
        return wbuf.at[b, pl.ds(h * (4 // PIECES), 4 // PIECES), pl.ds(pl.multiple_of(owner * slab, slab), slab), :]

    def wcopy(b, h, owner, to, sem):
        return pltpu.make_async_remote_copy(
            src_ref=place(b, h, owner),
            dst_ref=place(b, h, owner),
            send_sem=sem, recv_sem=wr.at[b, h, owner],
            device_id={"loop": to}, device_id_type=MESH)

    def got(b, h, owner):
        wcopy(b, h, owner, lax.rem(me + 1, peers), wp.at[b, h, 0]).wait_recv()

    def along(b, h, s, act_on):
        zp = plane(s)
        owner = index(zp, x, c)

        @pl.when((zp <= z) & (z < zs - 1))
        def _():
            act_on(wcopy(b, h, owner, index(lax.rem(z + 1, zs), x, c), wu.at[b, h, s]))

        @pl.when((zp >= z) & (z > 0))
        def _():
            act_on(wcopy(b, h, owner, index(lax.rem(z + zs - 1, zs), x, c), wd.at[b, h, s]))

    edge = jnp.where(z % 2 == 0, z + 1, z - 1)
    outer = (z == 0) | (z == zs - 1)

    def by_edge(b, h, corner):
        return (b, h) in (TO_INNER if corner else TO_OUTER)

    def over_x(b, h, s):
        may = not isinstance(s, int) or s == 1
        skip_outer = may and by_edge(b, h, False)
        skip_inner = may and by_edge(b, h, True)
        keep = z >= 0
        if skip_outer:
            keep = keep & jnp.logical_not(outer & (s == 1))
        if skip_inner:
            keep = keep & (outer | (s != 1))
        return keep

    def across(b, h, s, act_on):
        owner = index(plane(s), x, c)

        @pl.when(over_x(b, h, s))
        def _():
            for j in range(1, xs):
                act_on(wcopy(b, h, owner, index(z, lax.rem(x + j, xs), c), wx.at[b, h, s * (xs - 1) + j - 1]))

        act_on(wcopy(b, h, owner, index(z, x, 1 - c), wp.at[b, h, s]))

    def past_edge(b, h, act_on):
        if not by_edge(b, h, True) and not by_edge(b, h, False):
            return
        copy = wcopy(b, h, index(z, 1 - x, c), index(edge, x, c), we.at[b, h])
        if by_edge(b, h, True):
            @pl.when(outer)
            def _():
                act_on(copy)
        if by_edge(b, h, False):
            @pl.when(jnp.logical_not(outer))
            def _():
                act_on(copy)

    def start(copy):
        copy.start()

    def sent(copy):
        copy.wait_send()

    def forward_column(b, s):
        for h in range(PIECES):
            got(b, h, index(plane(s), x, c))
            along(b, h, s, start)
            across(b, h, s, start)

    def to_partner(b, h, s, j):
        owner = index(plane(s), lax.rem(x + j, xs), c)
        return wcopy(b, h, owner, index(z, x, 1 - c), wq.at[b, h, s * (xs - 1) + j - 1])

    def forward_across(b, s):
        for h in range(PIECES):
            for j in range(1, xs):
                got(b, h, index(plane(s), lax.rem(x + j, xs), c))

                @pl.when(s == 0)
                def _():
                    past_edge(b, h, start)

                to_partner(b, h, s, j).start()

    def arrived(b, s):
        for h in range(PIECES):
            for j in range(xs):
                got(b, h, index(plane(s), j, 1 - c))

    def ycopy(b, s):
        return pltpu.make_async_remote_copy(
            src_ref=psend.at[b, s], dst_ref=precv.at[b, s],
            send_sem=ys.at[b, s], recv_sem=yr.at[b, s],
            device_id={"ch": 1 - half}, device_id_type=MESH)

    def chunk_of(s):
        return pl.ds(pl.multiple_of(plane(s) * chunk, chunk), chunk)

    nt = (((1,), (1,)), ((), ()))
    tn = (((0,), (0,)), ((), ()))

    def middle(b, s):
        at = chunk_of(s)
        shift = (b + 1) * part
        total = None
        for t in range(3):
            term = lax.dot_general(
                wbuf[b, t, at, :], act[pl.ds(pad + (t - 1) * shift, rows), :], nt,
                preferred_element_type=jnp.float32)
            total = term if total is None else total + term
        mid[s] = total
        psend[b, s] = total.astype(jnp.bfloat16)
        ycopy(b, s).start()

    def project(b, s, first=False):
        at = chunk_of(s)
        ycopy(b, s).wait_recv()
        total = mid[s] + precv[b, s].astype(jnp.float32)
        hid = gelu(total * cols[at, pl.ds(b, 1)] + cols[at, pl.ds(2 + b, 1)]).astype(jnp.bfloat16)
        term = lax.dot_general(hid, wbuf[b, 3, at, :], tn, preferred_element_type=jnp.float32)
        if first:
            acc[...] = term
        else:
            acc[...] += term

    step = 64 if rows % 64 == 0 else part

    def activate(src):
        @pl.loop(0, rows // step)
        def _(i):
            at = pl.ds(pl.multiple_of(i * step, step), step)
            act[pl.ds(pl.multiple_of(pad + i * step, part), step), :] = gelu(
                src[at, :].astype(jnp.float32)).astype(jnp.bfloat16)

        wrap()

    def wrap():
        act[pl.ds(0, pad), :] = act[pl.ds(rows, pad), :]
        act[pl.ds(pad + rows, pad), :] = act[pl.ds(pad, pad), :]

    def advance():
        @pl.loop(0, rows // step)
        def _(i):
            at = pl.ds(pl.multiple_of(i * step, step), step)
            new = (
                state[at, :].astype(jnp.float32)
                + acc[at, :] * os_ref[pl.ds(0, 1), :] + ot_ref[pl.ds(0, 1), :]
            ).astype(jnp.bfloat16)
            state[at, :] = new
            act[pl.ds(pl.multiple_of(pad + i * step, part), step), :] = gelu(
                new.astype(jnp.float32)).astype(jnp.bfloat16)

        wrap()

    def finish(first, count):
        at = pl.ds(pl.multiple_of(first * part, part), count * part)
        res[at, :] = (
            state[at, :].astype(jnp.float32) + acc[at, :] * os_ref[pl.ds(1, 1), :] + ot_ref[pl.ds(1, 1), :]
        ).astype(jnp.bfloat16)

    own_x = pltpu.make_async_copy(x_ref.at[rowset(me)], state.at[rowset(me)], loc.at[0])
    own_w = []
    for b in range(2):
        at = pl.ds(pl.multiple_of(me * slab, slab), slab)
        own_w.append(pltpu.make_async_copy(k_ref.at[b], wbuf.at[b, pl.ds(0, 3), at, :], loc.at[1 + 2 * b]))
        own_w.append(pltpu.make_async_copy(p_ref.at[b], wbuf.at[b, 3, at, :], loc.at[2 + 2 * b]))

    barrier = pltpu.get_barrier_semaphore()

    @pl.loop(1, peers)
    def _(i):
        pl.semaphore_signal(barrier, inc=1, device_id={"loop": lax.rem(me + i, peers)}, device_id_type=MESH)

    pl.semaphore_signal(barrier, inc=1, device_id={"ch": 1 - half}, device_id_type=MESH)
    for copy in own_w:
        copy.start()
    own_x.start()
    coef[...] = jnp.zeros_like(coef)
    small = [
        pltpu.make_async_copy(ms_ref, coef.at[pl.ds(0, 2)], loc.at[5]),
        pltpu.make_async_copy(mt_ref, coef.at[pl.ds(2, 2)], loc.at[6]),
        pltpu.make_async_copy(osh_ref, os_ref, loc.at[7]),
        pltpu.make_async_copy(oth_ref, ot_ref, loc.at[8]),
    ]
    for copy in small:
        copy.start()
    acc[...] = jnp.zeros_like(acc)
    for copy in own_w:
        copy.wait()
    own_x.wait()
    for copy in small:
        copy.wait()
    cols[...] = coef[...].T
    pl.semaphore_wait(barrier, peers)

    def own_slab(b):
        for h in range(PIECES):
            along(b, h, 0, start)
            across(b, h, 0, start)

    inner = jnp.logical_not(outer)

    own_slab(0)
    to_all(a2a_in)
    for h in range(PIECES):
        across(1, h, 0, start)

        @pl.when(outer)
        def _():
            along(1, h, 0, start)

    forward_column(0, 1)

    @pl.when(inner)
    def _():
        forward_column(0, 2)

    forward_across(0, 0)

    @pl.loop(1, peers)
    def _(i):
        a2a_in_recv(i).wait_recv()

    activate(state)

    @pl.loop(0, zs + 1)
    def _(s):
        @pl.when(s < zs)
        def _():
            @pl.when(s > 0)
            def _():
                forward_across(0, s)

            arrived(0, s)
            middle(0, s)

        @pl.when(outer & (s == 0))
        def _():
            forward_column(0, 2)

        @pl.when(inner & (s == 0))
        def _():
            along(1, 0, 0, start)

        @pl.when((outer & (s == 1)) | (inner & (s == 0)))
        def _():
            forward_column(0, 3)

        @pl.when(inner & (s == 0))
        def _():
            along(1, 1, 0, start)

        @pl.when((outer & (s == 2)) | (inner & (s == 1)))
        def _():
            forward_across(1, 0)
            forward_column(1, 1)

        @pl.when(inner & (s == 2))
        def _():
            forward_column(1, 2)

        @pl.when(inner & (s == 3))
        def _():
            forward_column(1, 3)

        @pl.when(s > 0)
        def _():
            project(0, s - 1)

        @pl.when(outer & (s == 3))
        def _():
            forward_column(1, 2)

    advance()

    last = zs - 1

    @pl.loop(0, last)
    def _(s):
        @pl.when(s > 0)
        def _():
            forward_across(1, s)

        arrived(1, s)
        middle(1, s)

        @pl.when(outer & (s == 1))
        def _():
            forward_column(1, 3)

    project(1, 0, first=True)

    forward_across(1, last)
    arrived(1, last)
    group = CORES * xs
    level = group * part
    far = jnp.where(z < zs // 2, 1, 0)
    span = rows // HALVES
    last_at = chunk_of(last)
    shift = 2 * part

    def halfset(q):
        return pl.ds(pl.multiple_of(q * span, span), span)

    def lcopy(k):
        return pltpu.make_async_remote_copy(
            src_ref=lsend.at[k], dst_ref=lrecv.at[k],
            send_sem=yls.at[k], recv_sem=ylr.at[k],
            device_id={"ch": 1 - half}, device_id_type=MESH)

    def to_half(k):
        return jnp.where(far == 1, 1 - k, k) if HALVES == 2 else k

    for k in range(HALVES):
        q = to_half(k)
        total = None
        for t in range(3):
            term = lax.dot_general(
                wbuf[1, t, last_at, :],
                act[pl.ds(pl.multiple_of(pad + (t - 1) * shift + q * span, part), span), :], nt,
                preferred_element_type=jnp.float32)
            total = term if total is None else total + term
        lmid[k] = total
        lsend[k] = total.astype(jnp.bfloat16)
        if k == 0:
            lcopy(k).start()

    project(1, last - 2)
    project(1, last - 1)
    lcopy(1).start()

    for k in range(HALVES):
        q = to_half(k)
        lcopy(k).wait_recv()
        total = lmid[k] + lrecv[k].astype(jnp.float32)
        hid = gelu(total * cols[last_at, pl.ds(1, 1)] + cols[last_at, pl.ds(3, 1)]).astype(jnp.bfloat16)
        acc[halfset(q), :] += lax.dot_general(hid, wbuf[1, 3, last_at, :], tn, preferred_element_type=jnp.float32)

        def send_level(zt):
            finish(zt * group, group)
            spot = lax.rem(me, group)
            for j in range(group):
                to = zt * group + lax.rem(spot + j, group)

                @pl.when(to != me)
                def _():
                    a2a_out(to).start()

        per = zs // HALVES

        @pl.loop(0, per)
        def _(i):
            at = jnp.where(z < zs // 2, per - 1 - i, i)
            send_level(q * per + at)

    own_o = pltpu.make_async_copy(res.at[rowset(me)], o_ref.at[rowset(me)], loc.at[0])
    own_o.start()
    own_o.wait()

    @pl.loop(1, peers)
    def _(i):
        a2a_out_recv(i).wait_recv()

    for b in range(2):
        for h in range(PIECES):
            along(b, h, 0, sent)
            across(b, h, 0, sent)
            past_edge(b, h, sent)

        @pl.loop(0, zs)
        def _(s):
            for h in range(PIECES):
                @pl.when(s > 0)
                def _():
                    along(b, h, s, sent)
                    across(b, h, s, sent)

                for j in range(1, xs):
                    to_partner(b, h, s, j).wait_send()

            @pl.when((s < zs - 1) | (b == 0))
            def _():
                ycopy(b, s).wait_send()

    for k in range(HALVES):
        lcopy(k).wait_send()

    @pl.loop(1, peers)
    def _(i):
        a2a_in(lax.rem(me + i, peers)).wait_send()
        a2a_out(lax.rem(me + i, peers)).wait_send()


def fused_shards(genome, kernel_w, point_w, mid_scale, mid_shift, out_scale, out_shift):
    peers = lax.axis_size("loop")
    rows, width = genome.shape
    slab = point_w.shape[1]
    mids = mid_scale.shape[1]
    xs = 2
    zs = peers // (CORES * xs)
    chunk = slab * CORES * xs
    part = rows // peers
    bf16, f32 = jnp.bfloat16, jnp.float32
    dma = pltpu.SemaphoreType.DMA
    hbm = pl.BlockSpec(memory_space=pltpu.HBM)
    vmem = pl.BlockSpec(memory_space=pltpu.VMEM)
    operands = (genome, jnp.swapaxes(kernel_w, 2, 3), point_w, mid_scale, mid_shift, out_scale, out_shift)
    return pl.pallas_call(
        functools.partial(kernel, peers, xs),
        out_shape=jax.ShapeDtypeStruct((rows, width), bf16),
        in_specs=[hbm] * len(operands),
        out_specs=vmem,
        scratch_shapes=[
            pltpu.VMEM((rows, width), bf16),
            pltpu.VMEM((rows + 4 * part, width), bf16),
            pltpu.VMEM((2, 4, mids, width), bf16),
            pltpu.VMEM((zs, chunk, rows), f32),
            pltpu.VMEM((2, zs, chunk, rows), bf16),
            pltpu.VMEM((2, zs, chunk, rows), bf16),
            pltpu.VMEM((rows, width), f32),
            pltpu.VMEM((rows, width), bf16),
            pltpu.VMEM((mids, 8), f32),
            pltpu.VMEM((8, mids), f32),
            pltpu.VMEM((2, width), f32),
            pltpu.VMEM((2, width), f32),
            pltpu.VMEM((HALVES, chunk, rows // HALVES), f32),
            pltpu.VMEM((HALVES, chunk, rows // HALVES), bf16),
            pltpu.VMEM((HALVES, chunk, rows // HALVES), bf16),
            dma((peers,)), dma((peers,)), dma((peers,)), dma((peers,)),
            dma((2, PIECES, peers)), dma((2, PIECES, zs)), dma((2, PIECES, zs * (xs - 1))),
            dma((2, PIECES, zs)), dma((2, PIECES, zs)), dma((2, PIECES, zs * (xs - 1))),
            dma((2, PIECES)), dma((2, zs)), dma((2, zs)), dma((HALVES,)), dma((HALVES,)), dma((9,)),
        ],
        compiler_params=pltpu.CompilerParams(
            collective_id=0, has_side_effects=True, vmem_limit_bytes=VMEM_BYTES),
    )(*(pltpu.with_memory_space_constraint(a, pltpu.HBM) for a in operands))


def shards(genome, kernel_w, *rest):
    peers = lax.axis_size("loop")
    rows, width = genome.shape
    slab = kernel_w.shape[3]
    fits = (
        peers == CORES * 2 * 4 and rows % (peers * TILE) == 0 and slab % TILE == 0
        and width % 128 == 0 and rows % 128 == 0 and lax.axis_size("ch") == 2
    )
    return (fused_shards if fits else plain_shards)(genome, kernel_w, *rest)


def solution(mesh):
    in_specs = (
        P("loop", "ch"),
        P(None, None, "ch", "loop"),
        P(None, "loop", "ch"),
        P(),
        P(),
        P(None, "ch"),
        P(None, "ch"),
    )
    return jax.shard_map(shards, mesh=mesh, in_specs=in_specs, out_specs=P("loop", "ch"), check_vma=False)
```
